32 devices in a mesh: seq: 8 (over z, x), tp: 4 (over y, core).
Axes of the slice: x: 2, y: 2, z: 4, core: 2. Of those that a mesh axis runs over, the one named last changes fastest.
Arguments:
- alignment: bfloat16 [16, 512, 768], P('seq', 'tp'), may hold values from -6 to 6
- gap_mask: int32 [16, 512], P('seq'), may hold values from 0 to 1, as said below
- weight_levels: int32 [16, 512], P('seq'), may hold values from 0 to 3
- true_cols: int32 [1], replicated, may hold values from 256 to 512
- cotangent: bfloat16 [16, 512, 768], P('seq', 'tp'), may hold values from -6 to 6
- gain_row: float32 [768], replicated, may hold values from 0.1 to 1.9
- row_query: bfloat16 [768, 768], P(None, 'tp'), may hold values from -0.3125 to 0.3125
- row_key: bfloat16 [768, 768], P(None, 'tp'), may hold values from -0.3125 to 0.3125
- row_value: bfloat16 [768, 768], P(None, 'tp'), may hold values from -0.21875 to 0.21875
- row_output: bfloat16 [768, 768], P('tp'), may hold values from -1.75 to 1.75
- gain_column: float32 [768], replicated, may hold values from 0.1 to 1.9
- column_query: bfloat16 [768, 768], P(None, 'tp'), may hold values from -0.21875 to 0.21875
- column_key: bfloat16 [768, 768], P(None, 'tp'), may hold values from -0.21875 to 0.21875
- column_value: bfloat16 [768, 768], P(None, 'tp'), may hold values from -0.21875 to 0.21875
- column_output: bfloat16 [768, 768], P('tp'), may hold values from -0.875 to 0.875
- gain_ffn: float32 [768], replicated, may hold values from 0.1 to 1.9
- ffn_in: bfloat16 [768, 3072], P(None, 'tp'), may hold values from -0.21875 to 0.21875
- ffn_out: bfloat16 [3072, 768], P('tp'), may hold values from -0.109375 to 0.109375
Outputs:
- result: bfloat16 [16, 512, 768], P('seq', 'tp')
- penalty: float32 [12], P('tp')
- alignment_grad: float32 [16, 512, 768], P('seq', 'tp')
- gain_row_grad: float32 [768], replicated
- row_query_grad: float32 [768, 768], P(None, 'tp')
- row_key_grad: float32 [768, 768], P(None, 'tp')
- row_value_grad: float32 [768, 768], P(None, 'tp')
- row_output_grad: float32 [768, 768], P('tp')
- gain_column_grad: float32 [768], replicated
- column_query_grad: float32 [768, 768], P(None, 'tp')
- column_key_grad: float32 [768, 768], P(None, 'tp')
- column_value_grad: float32 [768, 768], P(None, 'tp')
- column_output_grad: float32 [768, 768], P('tp')
- gain_ffn_grad: float32 [768], replicated
- ffn_in_grad: float32 [768, 3072], P(None, 'tp')
- ffn_out_grad: float32 [3072, 768], P('tp')
The draws below stay inside these ranges and needn't reach their ends.
Inputs may be any that keep to these rules, and one draw needn't show every extreme that they name: `gap_mask`: 1 marks a residue, 0 a gap. `weight_levels`: each level halves a token's weight. `true_cols`: columns at this index and beyond are padding.
All inputs are finite; a program needn't handle non-finite values.
Results may differ from the reference program's by a relative error of at most 0.024.
The reference program's roundings to bfloat16 on the way count: a program that leaves them out, or rounds other values in their place, can miss the bound.
Values may be sent and summed in bfloat16 or wider, within the bound.
No kernel may reach another device: no remote copies, remote signals or barrier semaphores. Data moves between devices by JAX's collectives and lax.ppermute only.
A program may use at most 384 MiB of HBM per device.

```python
import jax
import jax.numpy as jnp
from jax import lax

D = 768
H = 12
HD = 64
FF = 3072
COLS = 512
ROWS = 16


def draw_gap_mask(key, part):
    row_index = jnp.arange(ROWS, dtype=jnp.int32)
    threshold = 300 + 650 * row_index // max(ROWS - 1, 1)
    tickets = jax.random.randint(key, (ROWS, COLS), 0, 1000, dtype=jnp.int32)
    return (tickets < threshold[:, None]).astype(jnp.int32)


def set_ends(result, key, low, high):
    longest = result.shape.index(max(result.shape))
    spots = []
    for shift in (0, 1):
        where = [jax.random.randint(jax.random.fold_in(key, axis), (), 0, length) for axis, length in enumerate(result.shape)]
        where[longest] = (where[longest] + shift) % result.shape[longest]
        spots.append(tuple(where))
    return result.at[spots[0]].set(low).at[spots[1]].set(high)


def block_scale(key, extent, split, least, largest):
    loudness = 1.0
    for dim, shards_of in split:
        heights = jax.random.uniform(jax.random.fold_in(jax.random.fold_in(key, 6), dim), (shards_of,), jnp.float32, least / len(split), largest / len(split))
        loudness = loudness * jnp.repeat(jnp.exp(heights), extent[dim] // shards_of).reshape((-1,) + (1,) * (len(extent) - 1 - dim))
    return loudness


def scatter_about(rng, dims, deviation, bound, cuts=(), kind=jnp.bfloat16):
    drawn = deviation * jax.random.normal(rng, dims, jnp.float32)
    if cuts:
        drawn = drawn * block_scale(rng, dims, cuts, -0.22, 0.18)
    return jnp.clip(drawn, -bound, bound).astype(kind)


def setup_inputs(seed: int = 0) -> dict:
    key_of = jax.random.split(jax.random.key(seed), 19)
    return {
        "alignment": scatter_about(key_of[0], (ROWS, COLS, D), 1.0, 6.0, ((0, 8), (1, 4))),
        "gap_mask": draw_gap_mask(jax.random.fold_in(key_of[18], 71), 0),
        "weight_levels": set_ends(jax.random.randint(key_of[2], (ROWS, COLS), 0, 4), jax.random.fold_in(key_of[2], 1), 0, 3).astype(jnp.int32),
        "true_cols": jax.random.randint(key_of[3], (1,), COLS // 2, COLS + 1).astype(jnp.int32),
        "cotangent": scatter_about(key_of[4], (ROWS, COLS, D), 1.0, 6.0, ((0, 8), (1, 4))),
        "gain_row": jnp.clip(1.0 + 0.18 * jax.random.normal(key_of[5], (D,), jnp.float32), 0.1, 1.9),
        "row_query": scatter_about(key_of[6], (D, D), (D // 2) ** -0.5, 0.3125, ((1, 4),)),
        "row_key": scatter_about(key_of[7], (D, D), (D // 2) ** -0.5, 0.3125, ((1, 4),)),
        "row_value": scatter_about(key_of[8], (D, D), D ** -0.5, 0.21875, ((1, 4),)),
        "row_output": scatter_about(key_of[9], (D, D), (D // 64) ** -0.5, 1.75, ((0, 4),)),
        "gain_column": jnp.clip(1.0 + 0.18 * jax.random.normal(key_of[10], (D,), jnp.float32), 0.1, 1.9),
        "column_query": scatter_about(key_of[11], (D, D), D ** -0.5, 0.21875, ((1, 4),)),
        "column_key": scatter_about(key_of[12], (D, D), D ** -0.5, 0.21875, ((1, 4),)),
        "column_value": scatter_about(key_of[13], (D, D), D ** -0.5, 0.21875, ((1, 4),)),
        "column_output": scatter_about(key_of[14], (D, D), (D // 16) ** -0.5, 0.875, ((0, 4),)),
        "gain_ffn": jnp.clip(1.0 + 0.18 * jax.random.normal(key_of[15], (D,), jnp.float32), 0.1, 1.9),
        "ffn_in": scatter_about(key_of[16], (D, FF), D ** -0.5, 0.21875, ((1, 4),)),
        "ffn_out": scatter_about(key_of[17], (FF, D), FF ** -0.5, 0.109375, ((0, 4),)),
    }


NORM_EPSILON = 1e-05
ENTROPY_WEIGHT = 32.0
MASK_FILL = -1e+30
HIGHEST_PRECISION = lax.Precision.HIGHEST

@jax.custom_vjp
def low(v):
    return lax.optimization_barrier(v.astype(jnp.bfloat16)).astype(jnp.float32)

@jax.custom_vjp
def low_back(v):
    return v

def low_keep(v):
    return (low(v), None)

def low_pass(kept, grad):
    return (grad,)

def back_keep(v):
    return (v, None)

def back_low(kept, grad):
    return (low(grad),)
low.defvjp(low_keep, low_pass)
low_back.defvjp(back_keep, back_low)

def level_scale(levels):
    scaled = jnp.zeros(levels.shape, jnp.float32)
    for degree in range(4):
        scaled = scaled + jnp.where(levels == degree, 0.5 ** degree, 0.0).astype(jnp.float32)
    return scaled

def layer_norm(values, gain_vector):
    center = lax.optimization_barrier(jnp.mean(values, axis=-1, keepdims=True))
    offset = values - center
    spread = lax.optimization_barrier(jnp.mean(offset * offset, axis=-1, keepdims=True))
    return offset * lax.rsqrt(spread + NORM_EPSILON) * gain_vector

def project(values, matrix):
    return jnp.einsum('rcd,de->rce', values, matrix, precision=HIGHEST_PRECISION)

def block_forward(alignment, gain_row, row_query, row_key, row_value, row_output, gain_column, column_query, column_key, column_value, column_output, gain_ffn, ffn_in, ffn_out, token_scale, valid_keys, query_share, inv_norm):
    head_shape = (ROWS, COLS, H, HD)
    row_normed = low(layer_norm(alignment, gain_row))
    row_queries = low_back(low(project(row_normed, row_query) * token_scale[:, :, None])).reshape(head_shape)
    row_keys = low_back(low(project(row_normed, row_key) * token_scale[:, :, None])).reshape(head_shape)
    row_values = low_back(low(project(row_normed, row_value))).reshape(head_shape)
    raw_logits = low_back(jnp.einsum('rihe,rjhe->hij', row_queries, row_keys, precision=HIGHEST_PRECISION))
    logits = raw_logits * inv_norm
    masked = jnp.where(valid_keys[None, None, :], logits, MASK_FILL)
    row_attention = jax.nn.softmax(masked, axis=-1)
    log_total = jax.nn.logsumexp(masked, axis=-1)
    zeroed = jnp.where(valid_keys[None, None, :], logits, 0.0)
    entropy = log_total - lax.optimization_barrier(jnp.sum(row_attention * zeroed, axis=-1))
    penalty = lax.optimization_barrier(jnp.sum(entropy * query_share[None, :], axis=-1))
    row_mixture = low_back(low(jnp.einsum('hij,rjhe->rihe', low(row_attention), row_values, precision=HIGHEST_PRECISION))).reshape(ROWS, COLS, D)
    after_row = alignment + low_back(project(row_mixture, row_output))
    col_normed = low(layer_norm(after_row, gain_column))
    col_queries = low_back(low(project(col_normed, column_query))).reshape(head_shape)
    col_keys = low_back(low(project(col_normed, column_key))).reshape(head_shape)
    col_values = low_back(low(project(col_normed, column_value))).reshape(head_shape)
    scores = low_back(jnp.einsum('rche,sche->chrs', col_queries, col_keys, precision=HIGHEST_PRECISION) * HD ** (-0.5))
    col_attention = low(jax.nn.softmax(scores, axis=-1))
    col_mixture = low_back(low(jnp.einsum('chrs,sche->rche', col_attention, col_values, precision=HIGHEST_PRECISION))).reshape(ROWS, COLS, D)
    after_col = after_row + low_back(project(col_mixture, column_output))
    ffn_normed = low(layer_norm(after_col, gain_ffn))
    hidden = low_back(project(ffn_normed, ffn_in))
    active = low(jax.nn.gelu(hidden, approximate=False))
    outcome = after_col + low_back(project(active, ffn_out))
    return (outcome, penalty)

def reference(alignment, gap_mask, weight_levels, true_cols, cotangent, gain_row, row_query, row_key, row_value, row_output, gain_column, column_query, column_key, column_value, column_output, gain_ffn, ffn_in, ffn_out):
    token_scale = level_scale(weight_levels) * gap_mask.astype(jnp.float32)
    energy = jnp.sum(token_scale * token_scale) / COLS
    inv_norm = HD ** (-0.5) * lax.rsqrt(energy + NORM_EPSILON)
    positions = jnp.arange(COLS, dtype=jnp.int32)
    valid_keys = positions < true_cols[0]
    query_share = valid_keys.astype(jnp.float32) / true_cols[0].astype(jnp.float32)
    params = (alignment, gain_row, row_query, row_key, row_value, row_output, gain_column, column_query, column_key, column_value, column_output, gain_ffn, ffn_in, ffn_out)
    floats = tuple((element.astype(jnp.float32) for element in params))

    def forward(*inputs):
        return block_forward(*inputs, token_scale, valid_keys, query_share, inv_norm)
    (outcome, penalty), pullback = jax.vjp(forward, *floats)
    grads = pullback((cotangent.astype(jnp.float32), jnp.full((H,), ENTROPY_WEIGHT, jnp.float32)))
    return (outcome.astype(jnp.bfloat16), penalty, grads[0], grads[1], grads[2], grads[3], grads[4], grads[5], grads[6], grads[7], grads[8], grads[9], grads[10], grads[11], grads[12], grads[13])
```

```python
import jax
import jax.numpy as jnp
from jax import lax
from jax.experimental import pallas as pl
from jax.experimental.pallas import tpu as pltpu
from jax.sharding import PartitionSpec as P

HD = 64
NORM_EPSILON = 1e-05
ENTROPY_WEIGHT = 32.0
MASK_FILL = -1e30
BF = jnp.bfloat16
F32 = jnp.float32


def dot(a, b):
    return lax.dot_general(a, b, (((1,), (0,)), ((), ())), preferred_element_type=F32)


def dot_nt(a, b):
    return lax.dot_general(a, b, (((1,), (1,)), ((), ())), preferred_element_type=F32)


def dot_tn(a, b):
    return lax.dot_general(a, b, (((0,), (0,)), ((), ())), preferred_element_type=F32)


def call(name, body, args, outs, scalars=None, scratch=(), flops=0):
    n_in, n_out = len(args), len(outs)
    has = scalars is not None

    def kernel(*refs):
        refs = list(refs)
        sc = refs.pop(0) if has else None
        body(sc, refs[:n_in], refs[n_in : n_in + n_out], refs[n_in + n_out :])

    specs = [pl.BlockSpec(memory_space=pltpu.VMEM)] * n_in
    if has:
        specs = [pl.BlockSpec(memory_space=pltpu.SMEM)] + specs
    moved = sum(a.size * a.dtype.itemsize for a in args)
    shapes = [jax.ShapeDtypeStruct(s, d) for s, d in outs]
    moved += sum(o.size * o.dtype.itemsize for o in shapes)
    res = pl.pallas_call(
        kernel,
        out_shape=shapes,
        in_specs=specs,
        out_specs=[pl.BlockSpec(memory_space=pltpu.VMEM)] * n_out,
        scratch_shapes=list(scratch),
        name=name,
        cost_estimate=pl.CostEstimate(flops=flops, bytes_accessed=moved, transcendentals=0),
    )(*(([scalars] if has else []) + list(args)))
    return list(res)


def ln_parts(value):
    center = jnp.mean(value, axis=-1, keepdims=True)
    offset = value - center
    spread = jnp.mean(offset * offset, axis=-1, keepdims=True)
    inverse = lax.rsqrt(spread + NORM_EPSILON)
    return offset * inverse, inverse


def ln_back(upstream, value, gain):
    normed, inverse = ln_parts(value)
    scaled = upstream * gain
    mean_scaled = jnp.mean(scaled, axis=-1, keepdims=True)
    second = jnp.mean(scaled * normed, axis=-1, keepdims=True)
    return inverse * (scaled - mean_scaled - normed * second)


def total(refs):
    acc = refs[0][...].astype(F32)
    for r in refs[1:]:
        acc = acc + r[...].astype(F32)
    return acc


def join(refs):
    if len(refs) == 1:
        return refs[0][...].astype(F32)
    return jnp.concatenate([r[...].astype(F32) for r in refs], axis=0)


def swap(x, axis, n, mask):
    return lax.ppermute(x, axis, [(i, i ^ mask) for i in range(n)])


def tp_near(x):
    return swap(x, "tp", 4, 1)


def tp_far(x):
    return swap(x, "tp", 4, 2)


def tp_gather(x):
    far = tp_far(x)
    near = tp_near(x)
    return [x, near, far, tp_near(far)]


def tp_scatter(near_parts, far_parts):
    from_near = tp_near(near_parts[1])
    relay = tp_near(far_parts[1])
    both = (far_parts[0].astype(F32) + relay.astype(F32)).astype(BF)
    return [near_parts[0], from_near, tp_far(both)]


def shards(
    n_seq,
    n_tp,
    alignment,
    gap_mask,
    weight_levels,
    true_cols,
    cotangent,
    gain_row,
    row_query,
    row_key,
    row_value,
    row_output,
    gain_column,
    column_query,
    column_key,
    column_value,
    column_output,
    gain_ffn,
    ffn_in,
    ffn_out,
):
    assert n_tp == 4
    R, CL, D = alignment.shape
    COLS = gap_mask.shape[1]
    HW = row_query.shape[1]
    NH = HW // HD
    FW = ffn_in.shape[1]
    TOK = R * CL
    RE = R * HD
    CC = CL // n_seq
    IB = COLS // n_seq
    fast = n_seq == 8
    PT = R * CC
    s = lax.axis_index("seq")
    t = lax.axis_index("tp")
    col_shift = CL.bit_length() - 1
    info = jnp.stack([s, t, true_cols[0]]).astype(jnp.int32)
    gain = lambda g: g.reshape(1, D)
    tok = (TOK, D)

    def seq_send(pieces):
        return [pieces[0]] + [swap(pieces[m], "seq", n_seq, m) for m in range(1, n_seq)]

    def to_cols(pieces):
        if fast:
            return seq_send(pieces)
        x = pieces[0].reshape(R, n_seq, CC, D).swapaxes(0, 1).reshape(n_seq * PT, D)
        return [lax.all_to_all(x, "seq", 0, 0, tiled=True)]

    def to_rows(pieces):
        if fast:
            return seq_send(pieces)
        x = lax.all_to_all(pieces[0], "seq", 0, 0, tiled=True)
        return [x.reshape(n_seq, R, CC, D).swapaxes(0, 1).reshape(tok)]

    n_piece = n_seq if fast else 1
    piece_shape = (PT, D) if fast else tok

    def split_cols(sc, value, scratch, outs):
        if not fast:
            outs[0][...] = value.astype(BF)
            return
        scratch[...] = value.reshape(R, CL, D)
        for m in range(n_seq):
            at = pl.multiple_of((sc[0] ^ m) * CC, CC)
            outs[m][...] = scratch[:, pl.ds(at, CC), :].reshape(PT, D).astype(BF)

    def place_rows(sc, refs, scratch):
        if not fast:
            return refs[0][...].astype(F32)
        for m in range(n_seq):
            at = pl.multiple_of((sc[0] ^ m) * CC, CC)
            scratch[:, pl.ds(at, CC), :] = refs[m][...].astype(F32).reshape(R, CC, D)
        return scratch[...].reshape(tok)

    row_scratch = pltpu.VMEM((R, CL, D), F32)

    def reduce_rows(keep, sends):
        if not fast:
            x = lax.psum_scatter(keep[0], "seq", scatter_dimension=1, tiled=True)
            return [x]
        got = {m: swap(sends[m ^ 1], "seq", n_seq, 1) for m in (6, 2, 4, 0)}
        add = lambda *v: sum(e.astype(F32) for e in v).astype(BF)
        h6 = swap(add(keep[6], got[6]), "seq", n_seq, 2)
        h2 = swap(add(keep[2], got[2]), "seq", n_seq, 2)
        h4 = swap(add(keep[4], got[4], h6), "seq", n_seq, 4)
        return [keep[0], got[0], h2, h4]

    def gather_rows(block):
        if not fast:
            return [lax.all_gather(block, "seq", axis=1, tiled=True)]
        out = {0: block}
        out[4] = swap(block, "seq", n_seq, 4)
        out[2] = swap(block, "seq", n_seq, 2)
        out[1] = swap(block, "seq", n_seq, 1)
        out[6] = swap(out[4], "seq", n_seq, 2)
        for m in (2, 4, 6):
            out[m | 1] = swap(out[m], "seq", n_seq, 1)
        return [out[m] for m in range(n_seq)]

    def load_rows(sc, refs, h, scratch):
        if not fast:
            scratch[h] = refs[0][h]
            return
        for m in range(n_seq):
            at = pl.multiple_of((sc[0] ^ m) * IB, IB)
            scratch[h, pl.ds(at, IB), :] = refs[m][h]

    def butterfly(x, axis, n):
        m = 1
        while m < n:
            x = x + swap(x, axis, n, m)
            m *= 2
        return x

    def k_ln(sc, ins, outs, _):
        normed, _i = ln_parts(ins[0][...].astype(F32))
        outs[0][...] = (normed * ins[1][...]).astype(BF)

    align_tok = alignment.reshape(tok)
    (own_row,) = call("ln_row", k_ln, [align_tok, gain(gain_row)], [(tok, BF)])
    x_row = tp_gather(own_row)

    def k_split(sc, ins, outs, scratch):
        split_cols(sc, ins[0][...].astype(F32), scratch[0], outs)

    pieces = [(piece_shape, BF)] * n_piece
    align_c = to_cols(call("split_in", k_split, [align_tok], pieces, info, [row_scratch]))
    cot_c = to_cols(
        call("split_cot", k_split, [cotangent.reshape(tok)], pieces, info, [row_scratch])
    )
    own_cot = jnp.concatenate(cot_c, 0) if fast else cot_c[0]

    token_scale = jnp.zeros(weight_levels.shape, F32)
    for level in range(4):
        token_scale = token_scale + jnp.where(weight_levels == level, 0.5**level, 0.0)
    token_scale = token_scale * gap_mask.astype(F32)
    energy = jnp.full((8, 128), jnp.sum(token_scale * token_scale) / COLS, F32)
    energy = butterfly(energy, "seq", n_seq)
    by_block = token_scale.reshape(R, n_tp, CL)
    scales = [
        lax.dynamic_index_in_dim(by_block, t ^ k, 1, keepdims=False).reshape(TOK, 1)
        for k in range(n_tp)
    ]

    def heads_of(value):
        rows = [value[r * CL : (r + 1) * CL] for r in range(R)]
        return [
            jnp.concatenate([v[:, h * HD : (h + 1) * HD] for v in rows], axis=1) for h in range(NH)
        ]

    def tokens_of(head_list):
        return jnp.concatenate(
            [
                jnp.concatenate([v[:, r * HD : (r + 1) * HD] for v in head_list], axis=1)
                for r in range(R)
            ],
            axis=0,
        )

    def k_row_qkv(sc, ins, outs, _):
        n = len(outs)
        wq, wk, wv = (r[...] for r in ins[2 * n :])
        for p in range(n):
            x = ins[p][...]
            scale = ins[n + p][...]
            for a, (w, use) in enumerate(((wq, True), (wk, True), (wv, False))):
                y = dot(x, w)
                if use:
                    y = y * scale
                for h, piece in enumerate(heads_of(y)):
                    outs[p][a, h] = piece.astype(BF)

    qkv_shape = (3, NH, CL, RE)

    def row_qkv(ks):
        return call(
            "row_qkv",
            k_row_qkv,
            [x_row[k] for k in ks]
            + [scales[k] for k in ks]
            + [row_query, row_key, row_value],
            [(qkv_shape, BF)] * len(ks),
            flops=len(ks) * TOK * D * HW * 6,
        )

    row_heads = row_qkv((0, 1)) + row_qkv((2, 3))

    keep_masks = [m for m in range(n_seq) if m % 2 == 0] if fast else [0]
    send_masks = [m for m in range(n_seq) if m % 2 == 1] if fast else []
    blk = (NH, IB, COLS) if fast else (NH, COLS, COLS)

    def outer_blocks(sc, left, right, outs, full):
        for h in range(NH):
            prod = dot_nt(left(h), right(h))
            if not fast:
                outs[0][h] = prod
                continue
            full[...] = prod
            for o, m in zip(outs, keep_masks + send_masks):
                at = pl.multiple_of((sc[0] ^ m) * IB, IB)
                o[h] = full[pl.ds(at, IB), :].astype(o.dtype)

    def k_logits(sc, ins, outs, scratch):
        whole = lambda a, h: jnp.concatenate([r[a, h] for r in ins], axis=0)
        outer_blocks(sc, lambda h: whole(0, h), lambda h: whole(1, h), outs, scratch[0])

    block_outs = [(blk, F32)] * len(keep_masks) + [(blk, BF)] * len(send_masks)
    full_scratch = pltpu.VMEM((COLS, COLS), F32)
    cuts = call(
        "logits", k_logits, row_heads, block_outs, info, [full_scratch],
        flops=NH * COLS * COLS * RE * 2,
    )
    as_maps = lambda c: (
        dict(zip(keep_masks, c)),
        dict(zip(send_masks, c[len(keep_masks) :])),
    )
    logit_parts = reduce_rows(*as_maps(cuts))

    own = (NH, IB, COLS)

    def positions(sc, index):
        return ((sc[1] ^ (index >> col_shift)) << col_shift) + (index & (CL - 1))

    def valid_terms(sc, rows):
        limit = sc[2]
        keys = positions(sc, lax.broadcasted_iota(jnp.int32, (1, COLS), 1)) < limit
        mine = positions(sc, lax.broadcasted_iota(jnp.int32, (rows, 1), 0) + sc[0] * rows)
        share = jnp.where(mine < limit, 1.0, 0.0).astype(F32) / limit.astype(F32)
        return keys, share

    def k_softmax(sc, ins, outs, _):
        inv_norm = HD ** (-0.5) * lax.rsqrt(ins[0][0:1, 0:1] + NORM_EPSILON)
        keys, share = valid_terms(sc, IB)
        rows = []
        for h in range(NH):
            raw = ins[1][h].astype(F32)
            for r in ins[2:]:
                raw = raw + r[h].astype(F32)
            logits = raw * inv_norm
            masked = jnp.where(keys, logits, MASK_FILL)
            highest = jnp.max(masked, axis=-1, keepdims=True)
            unnormed = jnp.exp(masked - highest)
            totals = jnp.sum(unnormed, axis=-1, keepdims=True)
            attention = unnormed / totals
            zeroed = jnp.where(keys, logits, 0.0)
            entropy = highest + jnp.log(totals) - jnp.sum(attention * zeroed, -1, keepdims=True)
            outs[0][h] = attention.astype(BF)
            outs[1][h] = attention
            outs[2][h] = zeroed
            part = jnp.sum(entropy * share, axis=0, keepdims=True)
            rows.append(jnp.broadcast_to(part, (1, 128)))
        rows.append(jnp.zeros((8 - NH, 128), F32))
        outs[3][...] = jnp.concatenate(rows, axis=0)

    attn_own, attn_f32, zeroed, penalty_part = call(
        "softmax", k_softmax, [energy] + logit_parts,
        [(own, BF), (own, F32), (own, F32), ((8, 128), F32)], info,
    )
    attn_blocks = gather_rows(attn_own)

    parts4 = [(tok, BF)] * n_tp

    def k_row_mix(sc, ins, outs, _):
        nb = len(attn_blocks)
        heads = ins[nb : nb + n_tp]
        wo = ins[nb + n_tp][...]
        attn = outs[0]
        mixes = []
        for h in range(NH):
            load_rows(sc, ins[:nb], h, attn)
            values = jnp.concatenate([r[2, h] for r in heads], axis=0)
            mixes.append(dot(attn[h], values).astype(BF))
        for k in range(n_tp):
            mix = tokens_of([v[k * CL : (k + 1) * CL] for v in mixes])
            outs[1 + k][...] = mix
            outs[1 + n_tp + k][...] = dot(mix, wo).astype(BF)

    got = call(
        "row_mix", k_row_mix, attn_blocks + row_heads + [row_output],
        [((NH, COLS, COLS), BF)] + [((TOK, HW), BF)] * n_tp + parts4, info,
        flops=NH * COLS * COLS * RE * 2 + 4 * TOK * HW * D * 2,
    )
    attn_full, row_mix, out_parts = got[0], got[1 : 1 + n_tp], got[1 + n_tp :]
    branch = tp_scatter(out_parts[:2], out_parts[2:])

    def k_branch(sc, ins, outs, scratch):
        split_cols(sc, total(ins), scratch[0], outs)

    branch_c = to_cols(call("branch", k_branch, branch, pieces, info, [row_scratch]))

    def k_ln_col(sc, ins, outs, _):
        resid = join(ins[:n_piece]) + join(ins[n_piece : 2 * n_piece])
        outs[0][...] = resid
        normed, _i = ln_parts(resid)
        outs[1][...] = (normed * ins[-1][...]).astype(BF)

    after_row, own_col = call(
        "ln_col", k_ln_col, align_c + branch_c + [gain(gain_column)], [(tok, F32), (tok, BF)]
    )
    x_col = tp_gather(own_col)

    def same_column():
        a = lax.broadcasted_iota(jnp.int32, (TOK, TOK), 0)
        b = lax.broadcasted_iota(jnp.int32, (TOK, TOK), 1)
        return (a & (CC - 1)) == (b & (CC - 1))

    def col_attention(q, k, mask):
        scores = jnp.where(mask, dot_nt(q, k) * HD ** (-0.5), MASK_FILL)
        highest = jnp.max(scores, axis=-1, keepdims=True)
        unnormed = jnp.exp(scores - highest)
        return unnormed / jnp.sum(unnormed, axis=-1, keepdims=True)

    def head(value, h):
        return value[:, h * HD : (h + 1) * HD]

    def k_col(sc, ins, outs, _):
        n = len(outs) // 3
        wq, wk, wv, wo = (r[...] for r in ins[n:])
        mask = same_column()
        for p in range(n):
            x = ins[p][...]
            q, k, v = (dot(x, w).astype(BF) for w in (wq, wk, wv))
            for a, y in enumerate((q, k, v)):
                outs[p][a] = y
            mixes = [
                dot(col_attention(head(q, h), head(k, h), mask).astype(BF), head(v, h))
                for h in range(NH)
            ]
            mix = jnp.concatenate(mixes, axis=1).astype(BF)
            outs[n + p][...] = mix
            outs[2 * n + p][...] = dot(mix, wo).astype(BF)

    def col_forward(ks):
        n = len(ks)
        return call(
            "col_fwd", k_col,
            [x_col[k] for k in ks] + [column_query, column_key, column_value, column_output],
            [((3, TOK, HW), BF)] * n + [((TOK, HW), BF)] * n + [(tok, BF)] * n,
            flops=n * (TOK * D * HW * 8 + NH * TOK * TOK * HD * 4),
        )

    c01, c23 = col_forward((0, 1)), col_forward((2, 3))
    col_heads = c01[:2] + c23[:2]
    col_mix = c01[2:4] + c23[2:4]
    branch = tp_scatter(c01[4:], c23[4:])

    def k_ln_ffn(sc, ins, outs, _):
        resid = total(ins[:-1])
        outs[0][...] = resid
        normed, _i = ln_parts(resid)
        outs[1][...] = (normed * ins[-1][...]).astype(BF)

    after_col, own_ffn = call(
        "ln_ffn", k_ln_ffn, [after_row] + branch + [gain(gain_ffn)], [(tok, F32), (tok, BF)]
    )
    x_cot = tp_gather(own_cot)
    x_ffn = tp_gather(own_ffn)

    def k_ffn(sc, ins, outs, _):
        n = len(outs) // 4
        w_in, w_out = ins[2 * n][...], ins[2 * n + 1][...]
        for p in range(n):
            hidden = dot(ins[p][...], w_in)
            cdf = 0.5 * (1.0 + lax.erf(hidden * (0.5**0.5)))
            active = (hidden * cdf).astype(BF)
            density = jnp.exp(hidden * hidden * -0.5) * (0.5 / jnp.pi) ** 0.5
            slope = cdf + hidden * density
            grad_hidden = (dot_nt(ins[n + p][...], w_out) * slope).astype(BF)
            outs[p][...] = active
            outs[n + p][...] = grad_hidden
            outs[2 * n + p][...] = dot_nt(grad_hidden, w_in).astype(BF)
            outs[3 * n + p][...] = dot(active, w_out).astype(BF)

    def feed_forward(ks):
        n = len(ks)
        return call(
            "ffn", k_ffn,
            [x_ffn[k] for k in ks] + [x_cot[k] for k in ks] + [ffn_in, ffn_out],
            [((TOK, FW), BF)] * (2 * n) + [(tok, BF)] * (2 * n),
            flops=n * TOK * D * FW * 8,
        )

    f01, f23 = feed_forward((0, 1)), feed_forward((2, 3))
    active = f01[0:2] + f23[0:2]
    grad_hidden = f01[2:4] + f23[2:4]
    ups = tp_scatter(f01[4:6], f23[4:6])

    def k_ln_back(sc, ins, outs, _):
        grad = ln_back(total(ins[:3]), ins[3][...].astype(F32), ins[4][...]) + ins[5][...].astype(
            F32
        )
        for o in outs:
            if o.shape == tok:
                o[...] = grad.astype(o.dtype)
        small = [o for o in outs if o.shape != tok]
        for m, o in enumerate(small):
            o[...] = grad[m * PT : (m + 1) * PT].astype(BF)

    grad_after_col, own_gac = call(
        "ln_ffn_back", k_ln_back, ups + [after_col, gain(gain_ffn), own_cot],
        [(tok, F32), (tok, BF)],
    )
    x_gac = tp_gather(own_gac)

    out_sum = tp_scatter(f01[6:8], f23[6:8])

    def k_result(sc, ins, outs, _):
        value = total(ins).astype(BF)
        for m, o in enumerate(outs):
            o[...] = value[m * PT : (m + 1) * PT] if fast else value

    result_rows = to_rows(call("result", k_result, [after_col] + out_sum, pieces))

    def k_place(sc, ins, outs, scratch):
        outs[0][...] = place_rows(sc, ins, scratch[0]).astype(BF)

    (outcome,) = call("place_out", k_place, result_rows, [(tok, BF)], info, [row_scratch])

    def k_weight(sc, ins, outs, _):
        n = n_tp
        n_left = 1
        left = [r[...] for r in ins[:n]]
        right = [r[...] for r in ins[n : 2 * n]]
        acc = dot_tn(left[0], right[0])
        for a, b in zip(left[1:], right[1:]):
            acc = acc + dot_tn(a, b)
        outs[0][...] = acc.astype(BF)
        if len(outs) > 1:
            prod = acc * ins[2 * n][...].astype(F32)
            ones = jnp.ones((8, prod.shape[1]), F32)
            outs[1][...] = lax.dot_general(
                ones, prod, (((1,), (1,)), ((), ())),
                precision=lax.Precision.HIGHEST, preferred_element_type=F32,
            )

    def weight_grad(name, left, right, weight=None):
        rows, cols = left[0].shape[1], right[0].shape[1]
        outs = [((rows, cols), BF)] + ([((8, rows), F32)] if weight is not None else [])
        return call(
            name, k_weight, list(left) + list(right) + ([weight] if weight is not None else []),
            outs, flops=2 * rows * cols * TOK * n_tp,
        )

    (d_ffn_out,) = weight_grad("dw_ffn_out", active, x_cot)
    d_ffn_in, gain_ffn_part = weight_grad("dw_ffn_in", x_ffn, grad_hidden, ffn_in)

    def k_col_back(sc, ins, outs, _):
        n = len(outs) // 4
        wo, wq, wk, wv = (r[...] for r in ins[2 * n :])
        mask = same_column()
        for p in range(n):
            grad_mix = dot_nt(ins[p][...], wo).astype(BF)
            q, k, v = (ins[n + p][a] for a in range(3))
            dq, dk, dv = [], [], []
            for h in range(NH):
                attention = col_attention(head(q, h), head(k, h), mask)
                grad_attn = dot_nt(head(grad_mix, h), head(v, h))
                inner = jnp.sum(attention * grad_attn, axis=-1, keepdims=True)
                grad_scores = (attention * (grad_attn - inner)).astype(BF)
                dq.append(dot(grad_scores, head(k, h)) * HD ** (-0.5))
                dk.append(dot_tn(grad_scores, head(q, h)) * HD ** (-0.5))
                dv.append(dot_tn(attention.astype(BF), head(grad_mix, h)))
            acc = None
            for a, (d, w) in enumerate(((dq, wq), (dk, wk), (dv, wv))):
                y = jnp.concatenate(d, axis=1).astype(BF)
                outs[a * n + p][...] = y
                z = dot_nt(y, w)
                acc = z if acc is None else acc + z
            outs[3 * n + p][...] = acc.astype(BF)

    def col_backward(ks):
        n = len(ks)
        return call(
            "col_bwd", k_col_back,
            [x_gac[k] for k in ks] + [col_heads[k] for k in ks]
            + [column_output, column_query, column_key, column_value],
            [((TOK, HW), BF)] * (3 * n) + [(tok, BF)] * n,
            flops=n * (TOK * D * HW * 8 + NH * TOK * TOK * HD * 10),
        )

    b01, b23 = col_backward((0, 1)), col_backward((2, 3))
    d_col = [b01[2 * a : 2 * a + 2] + b23[2 * a : 2 * a + 2] for a in range(3)]
    ups = tp_scatter(b01[6:8], b23[6:8])
    gar_rows = to_rows(
        call(
            "ln_col_back", k_ln_back,
            ups + [after_row, gain(gain_column), grad_after_col],
            pieces,
        )
    )
    (own_gar,) = call("place_gar", k_place, gar_rows, [(tok, BF)], info, [row_scratch])
    x_gar = tp_gather(own_gar)

    (d_col_out,) = weight_grad("dw_col_out", col_mix, x_gac)
    d_col_q, gain_cq = weight_grad("dw_col_q", x_col, d_col[0], column_query)
    d_col_k, gain_ck = weight_grad("dw_col_k", x_col, d_col[1], column_key)
    d_col_v, gain_cv = weight_grad("dw_col_v", x_col, d_col[2], column_value)

    def k_row_back(sc, ins, outs, _):
        n = len(outs)
        wo = ins[n][...]
        for p in range(n):
            grad_mix = dot_nt(ins[p][...], wo)
            for h, piece in enumerate(heads_of(grad_mix)):
                outs[p][h] = piece.astype(BF)

    def row_back(ks):
        return call(
            "row_bwd", k_row_back, [x_gar[k] for k in ks] + [row_output],
            [((NH, CL, RE), BF)] * len(ks), flops=len(ks) * TOK * D * HW * 2,
        )

    grad_mix = row_back((0, 1)) + row_back((2, 3))

    def k_grad_attn(sc, ins, outs, scratch):
        left = lambda h: jnp.concatenate([r[h] for r in ins[:n_tp]], axis=0)
        right = lambda h: jnp.concatenate([r[2, h] for r in ins[n_tp:]], axis=0)
        outer_blocks(sc, left, right, outs, scratch[0])

    cuts = call(
        "grad_attn", k_grad_attn, grad_mix + row_heads, block_outs, info, [full_scratch],
        flops=NH * COLS * COLS * RE * 2,
    )
    attn_grad_parts = reduce_rows(*as_maps(cuts))

    def k_row_dv(sc, ins, outs, _):
        vals = []
        for h in range(NH):
            grads = jnp.concatenate([r[h] for r in ins[1:]], axis=0)
            vals.append(dot_tn(ins[0][h], grads).astype(BF))
        for k in range(n_tp):
            outs[k][...] = tokens_of([v[k * CL : (k + 1) * CL] for v in vals])

    d_row_v = call(
        "row_dv", k_row_dv, [attn_full] + grad_mix, [((TOK, HW), BF)] * n_tp,
        flops=NH * COLS * COLS * RE * 2,
    )
    (d_row_out,) = weight_grad("dw_row_out", row_mix, x_gar)
    d_row_value, gain_rv = weight_grad("dw_row_v", x_row, d_row_v, row_value)

    def k_softmax_back(sc, ins, outs, _):
        inv_norm = HD ** (-0.5) * lax.rsqrt(ins[0][0:1, 0:1] + NORM_EPSILON)
        _, share = valid_terms(sc, IB)
        for h in range(NH):
            grad = ins[3][h].astype(F32)
            for r in ins[4:]:
                grad = grad + r[h].astype(F32)
            attention = ins[1][h]
            shifted = grad - ENTROPY_WEIGHT * share * ins[2][h]
            inner = jnp.sum(attention * shifted, axis=-1, keepdims=True)
            outs[0][h] = (attention * (shifted - inner) * inv_norm).astype(BF)

    (graw_own,) = call(
        "softmax_back", k_softmax_back, [energy, attn_f32, zeroed] + attn_grad_parts,
        [(own, BF)], info,
    )
    graw_blocks = gather_rows(graw_own)

    def k_row_back2(sc, ins, outs, scratch):
        nb = len(graw_blocks)
        heads = ins[nb : nb + n_tp]
        scale = ins[nb + n_tp : nb + 2 * n_tp]
        dv = ins[nb + 2 * n_tp : nb + 3 * n_tp]
        wq, wk, wv = (r[...] for r in ins[nb + 3 * n_tp :])
        full = scratch[0]
        dq, dk = [], []
        for h in range(NH):
            load_rows(sc, ins[:nb], h, full)
            whole = lambda a: jnp.concatenate([r[a, h] for r in heads], axis=0)
            dq.append(dot(full[h], whole(1)).astype(BF))
            dk.append(dot_tn(full[h], whole(0)).astype(BF))
        for k in range(n_tp):
            acc = dot_nt(dv[k][...], wv)
            for a, (d, w) in enumerate(((dq, wq), (dk, wk))):
                y = tokens_of([v[k * CL : (k + 1) * CL] for v in d]).astype(F32) * scale[k][...]
                y = y.astype(BF)
                outs[a * n_tp + k][...] = y
                acc = acc + dot_nt(y, w)
            outs[2 * n_tp + k][...] = acc.astype(BF)

    got = call(
        "row_bwd2", k_row_back2,
        graw_blocks + row_heads + scales + d_row_v + [row_query, row_key, row_value],
        [((TOK, HW), BF)] * (2 * n_tp) + parts4, info,
        [pltpu.VMEM((NH, COLS, COLS), BF)],
        flops=NH * COLS * COLS * RE * 4 + 4 * TOK * HW * D * 6,
    )
    d_row_q, d_row_k, dx_parts = got[:n_tp], got[n_tp : 2 * n_tp], got[2 * n_tp :]
    d_row_query, gain_rq = weight_grad("dw_row_q", x_row, d_row_q, row_query)
    d_row_key, gain_rk = weight_grad("dw_row_k", x_row, d_row_k, row_key)
    ups = tp_scatter(dx_parts[:2], dx_parts[2:])
    (alignment_grad,) = call(
        "ln_row_back", k_ln_back, ups + [align_tok, gain(gain_row), own_gar], [(tok, F32)]
    )

    sums = lax.psum(
        (
            d_ffn_in, d_ffn_out,
            d_col_q, d_col_k, d_col_v, d_col_out,
            d_row_out, d_row_value, d_row_query, d_row_key,
        ),
        "seq",
    )
    sums = [v.astype(F32) for v in sums]
    pen = jnp.zeros((1, D), F32)
    pen = lax.dynamic_update_slice(pen, penalty_part[:NH, 0].reshape(1, NH), (0, t * NH))
    small = jnp.concatenate(
        [
            gain_ffn_part[:1] / gain(gain_ffn),
            (gain_cq[:1] + gain_ck[:1] + gain_cv[:1]) / gain(gain_column),
            (gain_rq[:1] + gain_rk[:1] + gain_rv[:1]) / gain(gain_row),
            pen,
        ],
        axis=0,
    )
    small = butterfly(butterfly(small, "tp", n_tp), "seq", n_seq)
    penalty = lax.dynamic_slice(small, (3, t * NH), (1, NH)).reshape(NH)
    back = (R, CL, D)
    return (
        outcome.reshape(back),
        penalty,
        alignment_grad.reshape(back),
        small[2],
        sums[8],
        sums[9],
        sums[7],
        sums[6],
        small[1],
        sums[2],
        sums[3],
        sums[4],
        sums[5],
        small[0],
        sums[0],
        sums[1],
    )


def solution(mesh):
    n_seq, n_tp = mesh.shape["seq"], mesh.shape["tp"]

    def body(*args):
        return shards(n_seq, n_tp, *args)

    weights_in = P(None, "tp")
    weights_out = P("tp", None)
    tokens = P("seq", "tp", None)
    return jax.shard_map(
        body,
        mesh=mesh,
        in_specs=(
            tokens, P("seq", None), P("seq", None), P(), tokens,
            P(), weights_in, weights_in, weights_in, weights_out,
            P(), weights_in, weights_in, weights_in, weights_out,
            P(), weights_in, weights_out,
        ),
        out_specs=(
            tokens, P("tp"), tokens,
            P(), weights_in, weights_in, weights_in, weights_out,
            P(), weights_in, weights_in, weights_in, weights_out,
            P(), weights_in, weights_out,
        ),
        check_vma=False,
    )
```
